32 devices in a mesh: rows: 8 (over z, x), tm: 4 (over y, core).
Axes of the slice: x: 2, y: 2, z: 4, core: 2. Of those that a mesh axis runs over, the one named last changes fastest.
Arguments:
- snapshots: bfloat16 [262144, 512], P('rows', 'tm'), may hold values from -6 to 6
- modes: bfloat16 [262144, 256], P('rows'), may hold values from -0.01171875 to 0.01171875
- eig_vectors: float32 [3, 256], replicated, may hold values from -0.375 to 0.375
- eig_values: float32 [3], replicated, may hold values from -1 to 1
Outputs:
- operator: float32 [256, 256], replicated
- eig_residual: float32 [3, 256], replicated
- residual_norm: float32 [3], replicated
The draws below stay inside these ranges and needn't reach their ends.
All inputs are finite; a program needn't handle non-finite values.
Results may differ from the reference program's by a relative error of at most 0.0003.
Values may be sent and summed in bfloat16 or wider, within the bound.
A program may use at most 128 MiB of HBM per device.

```python
import jax
import jax.numpy as jnp
from jax import lax

M_DEV = 32768
R = 256
EIGS = 3
ROWS_ALL = 262144
TIMES = 512
N_ROWS = 8


def steps_of(key, dims, shards, least, top_value):
    level = 1.0
    for position, blocks in shards:
        heights = jax.random.uniform(jax.random.fold_in(jax.random.fold_in(key, 6), position), (blocks,), jnp.float32, least / len(shards), top_value / len(shards))
        level = level * jnp.repeat(jnp.exp(heights), dims[position] // blocks).reshape((-1,) + (1,) * (len(dims) - 1 - position))
    return level


def normal_values(stream_key, dims, scale, reach, shards=(), held_as=jnp.bfloat16):
    array = scale * jax.random.normal(stream_key, dims, jnp.float32)
    if shards:
        array = array * steps_of(stream_key, dims, shards, -0.22, 0.18)
    return jnp.clip(array, -reach, reach).astype(held_as)


def setup_inputs(seed: int = 0) -> dict:
    key_of = jax.random.split(jax.random.key(seed), 5)
    snapshots = normal_values(key_of[0], (ROWS_ALL, TIMES), 1.0, 6.0, ((0, 8), (1, 4)))
    modes = normal_values(key_of[1], (ROWS_ALL, R), ROWS_ALL ** -0.5, 0.01171875, ((0, 8),))
    eig_vectors = normal_values(key_of[2], (EIGS, R), R ** -0.5, 0.375, (), jnp.float32)
    eig_values = jnp.clip(jax.random.uniform(key_of[3], (EIGS,), jnp.float32, -1.0, 1.0), -1.0, 1.0)
    return {"snapshots": snapshots, "modes": modes, "eig_vectors": eig_vectors, "eig_values": eig_values}


def reference(snapshots, modes, eig_vectors, eig_values):
    blocks_x = snapshots.reshape(N_ROWS, M_DEV, TIMES)
    blocks_u = modes.reshape(N_ROWS, M_DEV, R)

    def accumulate(total, pair):
        basis, data = pair
        term = jnp.dot(basis.astype(jnp.float32).T.astype(jnp.float32), data.astype(jnp.float32), precision=lax.Precision.HIGHEST, preferred_element_type=jnp.float32)
        return (total + term, None)
    coords, _ = lax.scan(accumulate, jnp.zeros((R, TIMES), jnp.float32), (blocks_u, blocks_x))
    lead = coords[:, :-1]
    trail = coords[:, 1:]
    scale = jnp.float32(TIMES - 1)
    cross = jnp.dot(trail.astype(jnp.float32), lead.T.astype(jnp.float32), precision=lax.Precision.HIGHEST, preferred_element_type=jnp.float32) / scale
    gram = jnp.dot(lead.astype(jnp.float32), lead.T.astype(jnp.float32), precision=lax.Precision.HIGHEST, preferred_element_type=jnp.float32) / scale + jnp.eye(R, dtype=jnp.float32)
    operator = jnp.linalg.solve(gram, cross.T).T
    eig_residual = jnp.dot(eig_vectors.astype(jnp.float32), operator.T.astype(jnp.float32), precision=lax.Precision.HIGHEST, preferred_element_type=jnp.float32) - eig_values[:, None] * eig_vectors
    residual_norm = jnp.sqrt(lax.optimization_barrier(jnp.sum(eig_residual * eig_residual, axis=1)) + 1e-06)
    return (operator, eig_residual, residual_norm)
```

```python
import functools

import jax
import jax.numpy as jnp
from jax import lax
from jax.experimental import pallas as pl
from jax.experimental.pallas import tpu as pltpu
from jax.sharding import PartitionSpec as P

MESH = pl.DeviceIdType.MESH
HIGHEST = lax.Precision.HIGHEST
NT = (((1,), (1,)), ((), ()))
NN = (((1,), (0,)), ((), ()))
CHUNKS = 16
CORES = 2


def gather_kernel(n, m, snap_hbm, modes_hbm, full, snap, basis, partial, landed, acc,
                  snap_sem, basis_sem, rs_send, rs_recv, ag_send, y_send, c_send, ag_recv):
    r = lax.axis_index("rows")
    t = lax.axis_index("tm")
    chips = m // CORES
    y, core = t // CORES, t % CORES
    twin = y * CORES + (1 - core)
    chunk = snap.shape[0] // CHUNKS
    piece = full.shape[1] // n

    def load(i):
        span = pl.ds(i * chunk, chunk)
        return (
            pltpu.make_async_copy(snap_hbm.at[span], snap.at[span], snap_sem.at[i]),
            pltpu.make_async_copy(modes_hbm.at[span], basis.at[span], basis_sem.at[i]),
        )

    for i in range(CHUNKS):
        for copy in load(i):
            copy.start()

    def row_peer(k):
        return lax.rem(r + k, n)

    def y_peer(d):
        return lax.rem(y + d, chips) * CORES + core

    barrier = pltpu.get_barrier_semaphore()
    for k in range(1, n):
        pl.semaphore_signal(barrier, inc=1, device_id=(row_peer(k), t), device_id_type=MESH)
    for d in range(1, chips):
        pl.semaphore_signal(barrier, inc=1, device_id=(r, y_peer(d)), device_id_type=MESH)
    pl.semaphore_signal(barrier, inc=1, device_id=(r, twin), device_id_type=MESH)

    acc[...] = jnp.zeros_like(acc)
    for i in range(CHUNKS):
        for copy in load(i):
            copy.wait()
        span = pl.ds(i * chunk, chunk)
        acc[...] += lax.dot_general(
            snap[span, :], basis[span, :], (((0,), (0,)), ((), ())),
            preferred_element_type=jnp.float32,
        )
    partial[...] = acc[...].T

    pl.semaphore_wait(barrier, n - 1 + chips - 1 + 1)

    def rows_of(j):
        return pl.ds(pl.multiple_of(j * piece, piece), piece)

    scatter = []
    for k in range(1, n):
        j = row_peer(k)
        copy = pltpu.make_async_remote_copy(
            src_ref=partial.at[rows_of(j)], dst_ref=landed.at[n - k],
            send_sem=rs_send.at[k], recv_sem=rs_recv.at[n - k],
            device_id=(j, t), device_id_type=MESH,
        )
        copy.start()
        scatter.append(copy)

    def arrival(k):
        return pltpu.make_async_remote_copy(
            src_ref=landed.at[k], dst_ref=landed.at[k],
            send_sem=rs_send.at[k], recv_sem=rs_recv.at[k],
            device_id=(row_peer(k), t), device_id_type=MESH,
        )

    total = partial[rows_of(r), :]
    for k in range(1, n):
        arrival(k).wait_recv()
        total = total + landed[k]
    full[t, rows_of(r), :] = total

    def send(block, j, sem, to):
        return pltpu.make_async_remote_copy(
            src_ref=full.at[block, rows_of(j)], dst_ref=full.at[block, rows_of(j)],
            send_sem=sem, recv_sem=ag_recv.at[block, j],
            device_id=to, device_id_type=MESH,
        )

    started = []

    def go(copy):
        copy.start()
        started.append(copy)

    for k in range(1, n):
        go(send(t, r, ag_send.at[k], (row_peer(k), t)))
    for k in range(n):
        j = row_peer(n - k) if k else r
        if k:
            send(t, j, ag_send.at[k], (j, t)).wait_recv()
        for d in range(1, chips):
            go(send(t, j, y_send.at[d, k], (r, y_peer(d))))
        go(send(t, j, c_send.at[0, k], (r, twin)))
    for d in range(1, chips):
        block = y_peer(chips - d)
        for k in range(n):
            j = row_peer(n - k) if k else r
            send(block, j, y_send.at[d, k], (r, block)).wait_recv()
            go(send(block, j, c_send.at[d, k], (r, twin)))
    for d in range(chips):
        block = lax.rem(y + d, chips) * CORES + (1 - core)
        for k in range(n):
            j = row_peer(k) if k else r
            send(block, j, c_send.at[d, k], (r, twin)).wait_recv()
    for copy in scatter + started:
        copy.wait_send()


def gathered_coords(n, m, snapshots, modes):
    depth, block = snapshots.shape
    width = modes.shape[1]
    chips = m // CORES
    dma = pltpu.SemaphoreType.DMA
    return pl.pallas_call(
        functools.partial(gather_kernel, n, m),
        out_shape=jax.ShapeDtypeStruct((m, width, block), jnp.float32),
        in_specs=[pl.BlockSpec(memory_space=pl.ANY)] * 2,
        out_specs=pl.BlockSpec(memory_space=pltpu.VMEM),
        scratch_shapes=[
            pltpu.VMEM((depth, block), snapshots.dtype),
            pltpu.VMEM((depth, width), modes.dtype),
            pltpu.VMEM((width, block), jnp.float32),
            pltpu.VMEM((n, width // n, block), jnp.float32),
            pltpu.VMEM((block, width), jnp.float32),
            dma((CHUNKS,)),
            dma((CHUNKS,)),
            dma((n,)),
            dma((n,)),
            dma((n,)),
            dma((chips, n)),
            dma((chips, n)),
            dma((m, n)),
        ],
        compiler_params=pltpu.CompilerParams(
            collective_id=0, has_side_effects=True, vmem_limit_bytes=44 * 2**20
        ),
    )(snapshots, modes)


def solve_kernel(m, coords, vectors, values, operator, residual, norms, grams, work):
    width, block = coords.shape[1:]
    total = m * block
    scale = jnp.float32(total - 1)
    series = jnp.concatenate([coords[i] for i in range(m)], axis=1)
    column = lax.broadcasted_iota(jnp.int32, (width, total), 1)
    lead = jnp.where(column < total - 1, series, 0.0)
    trail = pltpu.roll(series, total - 1, 1)

    def exact(a, b, dims=NN):
        return lax.dot_general(a, b, dims, precision=HIGHEST, preferred_element_type=jnp.float32)

    def rough(a, b):
        return lax.dot_general(
            a.astype(jnp.bfloat16), b.astype(jnp.bfloat16), NN, preferred_element_type=jnp.float32
        )

    row = lax.broadcasted_iota(jnp.int32, (width, width), 0)
    col = lax.broadcasted_iota(jnp.int32, (width, width), 1)
    eye = jnp.where(row == col, 1.0, 0.0)
    cross = exact(trail, lead, NT) / scale
    gram = exact(lead, lead, NT) / scale + eye
    grams[0] = gram
    grams[1] = cross

    mean = jnp.sum(gram * eye) / width
    square = jnp.sum(gram * gram) / width
    spread = jnp.sqrt(jnp.full((1, 1), jnp.maximum(square - mean * mean, 0.0)))
    top = jnp.maximum(mean + 3.0 * spread, 1.001)
    middle, half = (top + 1.0) * 0.5, (top - 1.0) * 0.5
    guess = (2.0 * middle * eye - gram) * (2.0 / (2.0 * middle * middle - half * half))
    error = eye - rough(guess, gram)
    inverse = guess + rough(error, guess)
    error = rough(error, error)
    inverse = inverse + rough(error, inverse)
    error = rough(error, error)
    inverse = inverse + rough(error, inverse)
    grams[2] = inverse

    first = rough(cross, inverse)
    operator[...] = first
    rest = cross - exact(first, gram)
    grams[3] = rest

    def size(a):
        return jnp.sum(a * a)

    def more(state):
        step, left = state
        return jnp.logical_and(step < 6, jnp.logical_not(left <= 4e-10))

    def refine(state):
        step, _ = state
        better = operator[...] + rough(grams[3], grams[2])
        operator[...] = better
        rest = grams[1] - exact(better, grams[0])
        grams[3] = rest
        ratio = jnp.full((1, 1), size(rest)) / jnp.maximum(size(better), 1e-30)
        return step + 1, ratio[0, 0]

    _, left = lax.while_loop(more, refine, (jnp.int32(0), jnp.float32(1.0)))
    settled = left <= 4e-10

    @pl.when(settled)
    def _():
        operator[...] += rough(grams[3], grams[2])

    @pl.when(jnp.logical_not(settled))
    def _():
        work[pl.ds(0, width), :] = grams[0]
        work[pl.ds(width, width), :] = grams[1]
        lane = lax.broadcasted_iota(jnp.int32, (2 * width, width), 1)

        def eliminate(k, carry):
            whole = work[...]
            here = lane == k
            lever = jnp.sum(jnp.where(here, whole, 0.0), axis=1, keepdims=True)
            pivot_row = work[pl.ds(k, 1), :]
            pivot = jnp.sum(jnp.where(here[:1], pivot_row, 0.0), axis=1, keepdims=True)
            scaled = lever / pivot
            work[...] = jnp.where(here, scaled, whole - scaled * pivot_row)
            return carry

        lax.fori_loop(0, width, eliminate, 0)
        operator[...] = work[pl.ds(width, width), :]

    image = exact(vectors[...], operator[...], NT)
    count = vectors.shape[0]
    for k in range(count):
        line = image[k : k + 1, :] - values[k] * vectors[k : k + 1, :]
        residual[k : k + 1, :] = line
        length = jnp.sqrt(jnp.sum(line * line, axis=1, keepdims=True) + 1e-06)
        norms[k] = length[0, 0]


def solved(m, coords, vectors, values):
    width = coords.shape[1]
    vmem = pl.BlockSpec(memory_space=pltpu.VMEM)
    smem = pl.BlockSpec(memory_space=pltpu.SMEM)
    return pl.pallas_call(
        functools.partial(solve_kernel, m),
        out_shape=(
            jax.ShapeDtypeStruct((width, width), jnp.float32),
            jax.ShapeDtypeStruct(vectors.shape, jnp.float32),
            jax.ShapeDtypeStruct(values.shape, jnp.float32),
        ),
        in_specs=[vmem, vmem, smem],
        out_specs=(vmem, vmem, smem),
        scratch_shapes=[
            pltpu.VMEM((4, width, width), jnp.float32),
            pltpu.VMEM((2 * width, width), jnp.float32),
        ],
    )(coords, vectors, values)


def solution(mesh):
    n, m = mesh.shape["rows"], mesh.shape["tm"]

    def body(snapshots, modes, eig_vectors, eig_values):
        coords = gathered_coords(n, m, snapshots, modes)
        return solved(m, coords, eig_vectors, eig_values)

    return jax.shard_map(
        body,
        mesh=mesh,
        in_specs=(P("rows", "tm"), P("rows", None), P(), P()),
        out_specs=(P(), P(), P()),
        check_vma=False,
    )
```

```python
import functools

import jax
import jax.numpy as jnp
from jax import lax
from jax.experimental import pallas as pl
from jax.experimental.pallas import tpu as pltpu
from jax.sharding import PartitionSpec as P

MESH = pl.DeviceIdType.MESH
HIGHEST = lax.Precision.HIGHEST
NT = (((1,), (1,)), ((), ()))
NN = (((1,), (0,)), ((), ()))
CHUNKS = 16
CORES = 2


def gather_kernel(n, m, snap_hbm, modes_hbm, full, snap, basis, partial, landed, acc,
                  snap_sem, basis_sem, rs_send, rs_recv, ag_send, y_send, c_send, ag_recv):
    r = lax.axis_index("rows")
    t = lax.axis_index("tm")
    chips = m // CORES
    y, core = t // CORES, t % CORES
    twin = y * CORES + (1 - core)
    chunk = snap.shape[0] // CHUNKS
    piece = full.shape[1] // n

    def load(i):
        span = pl.ds(i * chunk, chunk)
        return (
            pltpu.make_async_copy(snap_hbm.at[span], snap.at[span], snap_sem.at[i]),
            pltpu.make_async_copy(modes_hbm.at[span], basis.at[span], basis_sem.at[i]),
        )

    for i in range(CHUNKS):
        for copy in load(i):
            copy.start()

    def row_peer(k):
        return lax.rem(r + k, n)

    def y_peer(d):
        return lax.rem(y + d, chips) * CORES + core

    barrier = pltpu.get_barrier_semaphore()
    for k in range(1, n):
        pl.semaphore_signal(barrier, inc=1, device_id=(row_peer(k), t), device_id_type=MESH)
    for d in range(1, chips):
        pl.semaphore_signal(barrier, inc=1, device_id=(r, y_peer(d)), device_id_type=MESH)
    pl.semaphore_signal(barrier, inc=1, device_id=(r, twin), device_id_type=MESH)

    acc[...] = jnp.zeros_like(acc)
    for i in range(CHUNKS):
        for copy in load(i):
            copy.wait()
        span = pl.ds(i * chunk, chunk)
        acc[...] += lax.dot_general(
            snap[span, :], basis[span, :], (((0,), (0,)), ((), ())),
            preferred_element_type=jnp.float32,
        )
    partial[...] = acc[...].T

    pl.semaphore_wait(barrier, n - 1 + chips - 1 + 1)

    def rows_of(j):
        return pl.ds(pl.multiple_of(j * piece, piece), piece)

    scatter = []
    for k in range(1, n):
        j = row_peer(k)
        copy = pltpu.make_async_remote_copy(
            src_ref=partial.at[rows_of(j)], dst_ref=landed.at[n - k],
            send_sem=rs_send.at[k], recv_sem=rs_recv.at[n - k],
            device_id=(j, t), device_id_type=MESH,
        )
        copy.start()
        scatter.append(copy)

    def arrival(k):
        return pltpu.make_async_remote_copy(
            src_ref=landed.at[k], dst_ref=landed.at[k],
            send_sem=rs_send.at[k], recv_sem=rs_recv.at[k],
            device_id=(row_peer(k), t), device_id_type=MESH,
        )

    total = partial[rows_of(r), :]
    for k in range(1, n):
        arrival(k).wait_recv()
        total = total + landed[k]
    full[t, rows_of(r), :] = total

    def send(block, j, sem, to):
        return pltpu.make_async_remote_copy(
            src_ref=full.at[block, rows_of(j)], dst_ref=full.at[block, rows_of(j)],
            send_sem=sem, recv_sem=ag_recv.at[block, j],
            device_id=to, device_id_type=MESH,
        )

    started = []

    def go(copy):
        copy.start()
        started.append(copy)

    for k in range(1, n):
        go(send(t, r, ag_send.at[k], (row_peer(k), t)))
    for k in range(n):
        j = row_peer(n - k) if k else r
        if k:
            send(t, j, ag_send.at[k], (j, t)).wait_recv()
        for d in range(1, chips):
            go(send(t, j, y_send.at[d, k], (r, y_peer(d))))
        go(send(t, j, c_send.at[0, k], (r, twin)))
    for d in range(1, chips):
        block = y_peer(chips - d)
        for k in range(n):
            j = row_peer(n - k) if k else r
            send(block, j, y_send.at[d, k], (r, block)).wait_recv()
            go(send(block, j, c_send.at[d, k], (r, twin)))
    for d in range(chips):
        block = lax.rem(y + d, chips) * CORES + (1 - core)
        for k in range(n):
            j = row_peer(k) if k else r
            send(block, j, c_send.at[d, k], (r, twin)).wait_recv()
    for copy in scatter + started:
        copy.wait_send()


def gathered_coords(n, m, snapshots, modes):
    depth, block = snapshots.shape
    width = modes.shape[1]
    chips = m // CORES
    dma = pltpu.SemaphoreType.DMA
    return pl.pallas_call(
        functools.partial(gather_kernel, n, m),
        out_shape=jax.ShapeDtypeStruct((m, width, block), jnp.float32),
        in_specs=[pl.BlockSpec(memory_space=pl.ANY)] * 2,
        out_specs=pl.BlockSpec(memory_space=pltpu.VMEM),
        scratch_shapes=[
            pltpu.VMEM((depth, block), snapshots.dtype),
            pltpu.VMEM((depth, width), modes.dtype),
            pltpu.VMEM((width, block), jnp.float32),
            pltpu.VMEM((n, width // n, block), jnp.float32),
            pltpu.VMEM((block, width), jnp.float32),
            dma((CHUNKS,)),
            dma((CHUNKS,)),
            dma((n,)),
            dma((n,)),
            dma((n,)),
            dma((chips, n)),
            dma((chips, n)),
            dma((m, n)),
        ],
        compiler_params=pltpu.CompilerParams(
            collective_id=0, has_side_effects=True, vmem_limit_bytes=60 * 2**20
        ),
    )(snapshots, modes)


def solve_kernel(m, coords, vectors, values, operator, residual, norms, grams, work):
    width, block = coords.shape[1:]
    total = m * block
    scale = jnp.float32(total - 1)
    series = jnp.concatenate([coords[i] for i in range(m)], axis=1)
    column = lax.broadcasted_iota(jnp.int32, (width, total), 1)
    lead = jnp.where(column < total - 1, series, 0.0)
    trail = pltpu.roll(series, total - 1, 1)

    def exact(a, b, dims=NN):
        return lax.dot_general(a, b, dims, precision=HIGHEST, preferred_element_type=jnp.float32)

    def rough(a, b):
        return lax.dot_general(
            a.astype(jnp.bfloat16), b.astype(jnp.bfloat16), NN, preferred_element_type=jnp.float32
        )

    row = lax.broadcasted_iota(jnp.int32, (width, width), 0)
    col = lax.broadcasted_iota(jnp.int32, (width, width), 1)
    eye = jnp.where(row == col, 1.0, 0.0)
    cross = exact(trail, lead, NT) / scale
    gram = exact(lead, lead, NT) / scale + eye
    grams[0] = gram
    grams[1] = cross

    mean = jnp.sum(gram * eye) / width
    square = jnp.sum(gram * gram) / width
    spread = jnp.sqrt(jnp.full((1, 1), jnp.maximum(square - mean * mean, 0.0)))
    top = jnp.maximum(mean + 3.0 * spread, 1.001)
    middle, half = (top + 1.0) * 0.5, (top - 1.0) * 0.5
    guess = (2.0 * middle * eye - gram) * (2.0 / (2.0 * middle * middle - half * half))
    error = eye - rough(guess, gram)
    inverse = guess + rough(error, guess)
    error = rough(error, error)
    inverse = inverse + rough(error, inverse)
    error = rough(error, error)
    inverse = inverse + rough(error, inverse)
    grams[2] = inverse

    first = rough(cross, inverse)
    operator[...] = first
    rest = cross - exact(first, gram)
    grams[3] = rest

    def size(a):
        return jnp.sum(a * a)

    def more(state):
        step, left = state
        return jnp.logical_and(step < 6, jnp.logical_not(left <= 1e-8))

    def refine(state):
        step, _ = state
        better = operator[...] + rough(grams[3], grams[2])
        operator[...] = better
        rest = grams[1] - exact(better, grams[0])
        grams[3] = rest
        ratio = jnp.full((1, 1), size(rest)) / jnp.maximum(size(better), 1e-30)
        return step + 1, ratio[0, 0]

    _, left = lax.while_loop(more, refine, (jnp.int32(0), jnp.float32(1.0)))
    settled = left <= 1e-8

    @pl.when(settled)
    def _():
        operator[...] += rough(grams[3], grams[2])

    @pl.when(jnp.logical_not(settled))
    def _():
        work[pl.ds(0, width), :] = grams[0]
        work[pl.ds(width, width), :] = grams[1]
        lane = lax.broadcasted_iota(jnp.int32, (2 * width, width), 1)

        def eliminate(k, carry):
            whole = work[...]
            here = lane == k
            lever = jnp.sum(jnp.where(here, whole, 0.0), axis=1, keepdims=True)
            pivot_row = work[pl.ds(k, 1), :]
            pivot = jnp.sum(jnp.where(here[:1], pivot_row, 0.0), axis=1, keepdims=True)
            scaled = lever / pivot
            work[...] = jnp.where(here, scaled, whole - scaled * pivot_row)
            return carry

        lax.fori_loop(0, width, eliminate, 0)
        operator[...] = work[pl.ds(width, width), :]

    image = exact(vectors[...], operator[...], NT)
    count = vectors.shape[0]
    for k in range(count):
        line = image[k : k + 1, :] - values[k] * vectors[k : k + 1, :]
        residual[k : k + 1, :] = line
        length = jnp.sqrt(jnp.sum(line * line, axis=1, keepdims=True) + 1e-06)
        norms[k] = length[0, 0]


def solved(m, coords, vectors, values):
    width = coords.shape[1]
    vmem = pl.BlockSpec(memory_space=pltpu.VMEM)
    smem = pl.BlockSpec(memory_space=pltpu.SMEM)
    return pl.pallas_call(
        functools.partial(solve_kernel, m),
        out_shape=(
            jax.ShapeDtypeStruct((width, width), jnp.float32),
            jax.ShapeDtypeStruct(vectors.shape, jnp.float32),
            jax.ShapeDtypeStruct(values.shape, jnp.float32),
        ),
        in_specs=[vmem, vmem, smem],
        out_specs=(vmem, vmem, smem),
        scratch_shapes=[
            pltpu.VMEM((4, width, width), jnp.float32),
            pltpu.VMEM((2 * width, width), jnp.float32),
        ],
    )(coords, vectors, values)


def solution(mesh):
    n, m = mesh.shape["rows"], mesh.shape["tm"]

    def body(snapshots, modes, eig_vectors, eig_values):
        coords = gathered_coords(n, m, snapshots, modes)
        return solved(m, coords, eig_vectors, eig_values)

    return jax.shard_map(
        body,
        mesh=mesh,
        in_specs=(P("rows", "tm"), P("rows", None), P(), P()),
        out_specs=(P(), P(), P()),
        check_vma=False,
    )
```

```python
import functools

import jax
import jax.numpy as jnp
from jax import lax
from jax.experimental import pallas as pl
from jax.experimental.pallas import tpu as pltpu
from jax.sharding import PartitionSpec as P

MESH = pl.DeviceIdType.MESH
HIGHEST = lax.Precision.HIGHEST
NT = (((1,), (1,)), ((), ()))
NN = (((1,), (0,)), ((), ()))
CHUNKS = 16
CORES = 2


def gather_kernel(n, m, snap_hbm, modes_hbm, full, snap, basis, partial, landed, acc,
                  snap_sem, basis_sem, rs_send, rs_recv, ag_send, y_send, c_send, ag_recv):
    r = lax.axis_index("rows")
    t = lax.axis_index("tm")
    chips = m // CORES
    y, core = t // CORES, t % CORES
    twin = y * CORES + (1 - core)
    chunk = snap.shape[0] // CHUNKS
    piece = full.shape[1] // n

    def load(i):
        span = pl.ds(i * chunk, chunk)
        return (
            pltpu.make_async_copy(snap_hbm.at[span], snap.at[span], snap_sem.at[i]),
            pltpu.make_async_copy(modes_hbm.at[span], basis.at[span], basis_sem.at[i]),
        )

    for i in range(CHUNKS):
        for copy in load(i):
            copy.start()

    def row_peer(k):
        return lax.rem(r + k, n)

    def y_peer(d):
        return lax.rem(y + d, chips) * CORES + core

    barrier = pltpu.get_barrier_semaphore()
    for k in range(1, n):
        pl.semaphore_signal(barrier, inc=1, device_id=(row_peer(k), t), device_id_type=MESH)
    for d in range(1, chips):
        pl.semaphore_signal(barrier, inc=1, device_id=(r, y_peer(d)), device_id_type=MESH)
    pl.semaphore_signal(barrier, inc=1, device_id=(r, twin), device_id_type=MESH)

    acc[...] = jnp.zeros_like(acc)
    for i in range(CHUNKS):
        for copy in load(i):
            copy.wait()
        span = pl.ds(i * chunk, chunk)
        acc[...] += lax.dot_general(
            snap[span, :], basis[span, :], (((0,), (0,)), ((), ())),
            preferred_element_type=jnp.float32,
        )
    partial[...] = acc[...].T

    pl.semaphore_wait(barrier, n - 1 + chips - 1 + 1)

    def rows_of(j):
        return pl.ds(pl.multiple_of(j * piece, piece), piece)

    scatter = []
    for k in range(1, n):
        j = row_peer(k)
        copy = pltpu.make_async_remote_copy(
            src_ref=partial.at[rows_of(j)], dst_ref=landed.at[n - k],
            send_sem=rs_send.at[k], recv_sem=rs_recv.at[n - k],
            device_id=(j, t), device_id_type=MESH,
        )
        copy.start()
        scatter.append(copy)

    def arrival(k):
        return pltpu.make_async_remote_copy(
            src_ref=landed.at[k], dst_ref=landed.at[k],
            send_sem=rs_send.at[k], recv_sem=rs_recv.at[k],
            device_id=(row_peer(k), t), device_id_type=MESH,
        )

    total = partial[rows_of(r), :]
    for k in range(1, n):
        arrival(k).wait_recv()
        total = total + landed[k]
    full[t, rows_of(r), :] = total

    def send(block, j, sem, to):
        return pltpu.make_async_remote_copy(
            src_ref=full.at[block, rows_of(j)], dst_ref=full.at[block, rows_of(j)],
            send_sem=sem, recv_sem=ag_recv.at[block, j],
            device_id=to, device_id_type=MESH,
        )

    started = []

    def go(copy):
        copy.start()
        started.append(copy)

    for k in range(n):
        j = row_peer(n - k) if k else r
        if k:
            send(t, j, ag_send.at[k], (j, t)).wait_recv()
        for d in range(1, chips):
            go(send(t, j, y_send.at[d, k], (r, y_peer(d))))
        go(send(t, j, c_send.at[0, k], (r, twin)))
        if k == 0:
            for hop in range(1, n):
                go(send(t, r, ag_send.at[hop], (row_peer(hop), t)))
    for d in range(1, chips):
        block = y_peer(chips - d)
        for k in range(n):
            j = row_peer(n - k) if k else r
            send(block, j, y_send.at[d, k], (r, block)).wait_recv()
            go(send(block, j, c_send.at[d, k], (r, twin)))
    for d in range(chips):
        block = lax.rem(y + d, chips) * CORES + (1 - core)
        for k in range(n):
            j = row_peer(k) if k else r
            send(block, j, c_send.at[d, k], (r, twin)).wait_recv()
    for copy in scatter + started:
        copy.wait_send()


def gathered_coords(n, m, snapshots, modes):
    depth, block = snapshots.shape
    width = modes.shape[1]
    chips = m // CORES
    dma = pltpu.SemaphoreType.DMA
    return pl.pallas_call(
        functools.partial(gather_kernel, n, m),
        out_shape=jax.ShapeDtypeStruct((m, width, block), jnp.float32),
        in_specs=[pl.BlockSpec(memory_space=pl.ANY)] * 2,
        out_specs=pl.BlockSpec(memory_space=pltpu.VMEM),
        scratch_shapes=[
            pltpu.VMEM((depth, block), snapshots.dtype),
            pltpu.VMEM((depth, width), modes.dtype),
            pltpu.VMEM((width, block), jnp.float32),
            pltpu.VMEM((n, width // n, block), jnp.float32),
            pltpu.VMEM((block, width), jnp.float32),
            dma((CHUNKS,)),
            dma((CHUNKS,)),
            dma((n,)),
            dma((n,)),
            dma((n,)),
            dma((chips, n)),
            dma((chips, n)),
            dma((m, n)),
        ],
        compiler_params=pltpu.CompilerParams(
            collective_id=0, has_side_effects=True, vmem_limit_bytes=60 * 2**20
        ),
    )(snapshots, modes)


def solve_kernel(m, coords, vectors, values, operator, residual, norms, grams, work):
    width, block = coords.shape[1:]
    total = m * block
    scale = jnp.float32(total - 1)
    series = jnp.concatenate([coords[i] for i in range(m)], axis=1)
    column = lax.broadcasted_iota(jnp.int32, (width, total), 1)
    lead = jnp.where(column < total - 1, series, 0.0)
    trail = pltpu.roll(series, total - 1, 1)

    def exact(a, b, dims=NN):
        return lax.dot_general(a, b, dims, precision=HIGHEST, preferred_element_type=jnp.float32)

    def rough(a, b):
        return lax.dot_general(
            a.astype(jnp.bfloat16), b.astype(jnp.bfloat16), NN, preferred_element_type=jnp.float32
        )

    row = lax.broadcasted_iota(jnp.int32, (width, width), 0)
    col = lax.broadcasted_iota(jnp.int32, (width, width), 1)
    eye = jnp.where(row == col, 1.0, 0.0)
    both = exact(jnp.concatenate([trail, lead], axis=0), lead, NT) / scale
    cross = both[:width]
    gram = both[width:] + eye
    grams[0] = gram
    grams[1] = cross

    mean = jnp.sum(gram * eye) / width
    square = jnp.sum(gram * gram) / width
    spread = jnp.sqrt(jnp.full((1, 1), jnp.maximum(square - mean * mean, 0.0)))
    top = jnp.maximum(mean + 3.0 * spread, 1.001)
    middle, half = (top + 1.0) * 0.5, (top - 1.0) * 0.5
    guess = (2.0 * middle * eye - gram) * (2.0 / (2.0 * middle * middle - half * half))
    error = eye - rough(guess, gram)
    inverse = guess + rough(error, guess)
    error = rough(error, error)
    inverse = inverse + rough(error, inverse)
    error = rough(error, error)
    inverse = inverse + rough(error, inverse)
    grams[2] = inverse

    first = rough(cross, inverse)
    operator[...] = first
    rest = cross - exact(first, gram)
    grams[3] = rest

    def size(a):
        return jnp.sum(a * a)

    def more(state):
        step, left = state
        return jnp.logical_and(step < 6, jnp.logical_not(left <= 1e-8))

    def refine(state):
        step, _ = state
        better = operator[...] + rough(grams[3], grams[2])
        operator[...] = better
        rest = grams[1] - exact(better, grams[0])
        grams[3] = rest
        ratio = jnp.full((1, 1), size(rest)) / jnp.maximum(size(better), 1e-30)
        return step + 1, ratio[0, 0]

    _, left = lax.while_loop(more, refine, (jnp.int32(0), jnp.float32(1.0)))
    settled = left <= 1e-8

    @pl.when(settled)
    def _():
        operator[...] += rough(grams[3], grams[2])

    @pl.when(jnp.logical_not(settled))
    def _():
        work[pl.ds(0, width), :] = grams[0]
        work[pl.ds(width, width), :] = grams[1]
        lane = lax.broadcasted_iota(jnp.int32, (2 * width, width), 1)

        def eliminate(k, carry):
            whole = work[...]
            here = lane == k
            lever = jnp.sum(jnp.where(here, whole, 0.0), axis=1, keepdims=True)
            pivot_row = work[pl.ds(k, 1), :]
            pivot = jnp.sum(jnp.where(here[:1], pivot_row, 0.0), axis=1, keepdims=True)
            scaled = lever / pivot
            work[...] = jnp.where(here, scaled, whole - scaled * pivot_row)
            return carry

        lax.fori_loop(0, width, eliminate, 0)
        operator[...] = work[pl.ds(width, width), :]

    image = exact(vectors[...], operator[...], NT)
    count = vectors.shape[0]
    for k in range(count):
        line = image[k : k + 1, :] - values[k] * vectors[k : k + 1, :]
        residual[k : k + 1, :] = line
        length = jnp.sqrt(jnp.sum(line * line, axis=1, keepdims=True) + 1e-06)
        norms[k] = length[0, 0]


def solved(m, coords, vectors, values):
    width = coords.shape[1]
    vmem = pl.BlockSpec(memory_space=pltpu.VMEM)
    smem = pl.BlockSpec(memory_space=pltpu.SMEM)
    return pl.pallas_call(
        functools.partial(solve_kernel, m),
        out_shape=(
            jax.ShapeDtypeStruct((width, width), jnp.float32),
            jax.ShapeDtypeStruct(vectors.shape, jnp.float32),
            jax.ShapeDtypeStruct(values.shape, jnp.float32),
        ),
        in_specs=[vmem, vmem, smem],
        out_specs=(vmem, vmem, smem),
        scratch_shapes=[
            pltpu.VMEM((4, width, width), jnp.float32),
            pltpu.VMEM((2 * width, width), jnp.float32),
        ],
    )(coords, vectors, values)


def solution(mesh):
    n, m = mesh.shape["rows"], mesh.shape["tm"]

    def body(snapshots, modes, eig_vectors, eig_values):
        coords = gathered_coords(n, m, snapshots, modes)
        return solved(m, coords, eig_vectors, eig_values)

    return jax.shard_map(
        body,
        mesh=mesh,
        in_specs=(P("rows", "tm"), P("rows", None), P(), P()),
        out_specs=(P(), P(), P()),
        check_vma=False,
    )
```
